32 devices in a mesh: tm: 8 (over z, x), frame: 4 (over y, core).
Axes of the slice: x: 2, y: 2, z: 4, core: 2. Of those that a mesh axis runs over, the one named last changes fastest.
Arguments:
- start_state: float32 [4, 32, 32, 128], P('frame'), may hold values from -6 to 6
- initial_guess: float32 [8, 4, 32, 32, 128], P('tm', 'frame'), may hold values from -6 to 6
- noise_draws: float32 [8, 4, 32, 32, 128], P('tm', 'frame'), may hold values from -6 to 6
- timesteps: int32 [8], P('tm'), may hold values from 0 to 999
- gain_space: float32 [128], replicated, may hold values from 0.1 to 1.9
- gain_attention: float32 [128], replicated, may hold values from 0.1 to 1.9
- time_weight: float32 [128, 256], replicated, may hold values from -0.5 to 0.5
- space_weight: bfloat16 [1152, 128], replicated, may hold values from -0.1875 to 0.1875
- attention_weight: bfloat16 [128, 384], replicated, may hold values from -4 to 4
- output_weight: bfloat16 [128, 128], replicated, may hold values from -0.5 to 0.5
Outputs:
- advanced: float32 [8, 4, 32, 32, 128], P('tm', 'frame')
The draws below stay inside these ranges and needn't reach their ends.
All inputs are finite; a program needn't handle non-finite values.
Results may differ from the reference program's by a relative error of at most 0.0025.
Values may be sent and summed in bfloat16 or wider, within the bound.
A program may use at most 64 MiB of HBM per device.

```python
import math
import jax
import jax.numpy as jnp
from jax import lax

C = 128
HEAD_DIM = 64
H = 32
W = 32
ITERS = 2
FRAMES = 4
STEPS = 8


def draw_attention_weight(key, part):
    drawn = jax.random.normal(jax.random.fold_in(key, 7), (C, 3 * C), jnp.float32) / math.sqrt(C)
    return jnp.clip(drawn, -4.0, 4.0).astype(jnp.bfloat16)


def touch_ends(values, stream_key, least, high):
    extent = values.shape
    index_at = [jax.random.randint(jax.random.fold_in(stream_key, axis), (), 0, extent[axis]) for axis in range(len(extent))]
    values = values.at[tuple(index_at)].set(least)
    longest = extent.index(max(extent))
    index_at[longest] = (index_at[longest] + 1) % extent[longest]
    return values.at[tuple(index_at)].set(high)


def shard_levels(own_key, extent, split, smallest, top_value):
    def one(position, parts):
        heights = jax.random.uniform(jax.random.fold_in(jax.random.fold_in(own_key, 6), position), (parts,), jnp.float32, smallest / len(split), top_value / len(split))
        return jnp.repeat(jnp.exp(heights), extent[position] // parts).reshape((-1,) + (1,) * (len(extent) - position - 1))

    level = one(*split[0])
    for cut in split[1:]:
        level = level * one(*cut)
    return level


def noise(key, extent, width, reach, pieces=(), kind=jnp.bfloat16):
    array = width * jax.random.normal(key, extent, jnp.float32)
    if pieces:
        array = array * shard_levels(key, extent, pieces, -0.22, 0.18)
    return jnp.clip(array, -reach, reach).astype(kind)


def setup_inputs(seed: int = 0) -> dict:
    keys = jax.random.split(jax.random.key(seed), 11)
    start_state = noise(keys[0], (FRAMES, H, W, C), 1.0, 6.0, ((0, 4),), jnp.float32)
    initial_guess = noise(keys[1], (STEPS, FRAMES, H, W, C), 1.0, 6.0, ((0, 8), (1, 4)), jnp.float32)
    noise_draws = noise(keys[2], (STEPS, FRAMES, H, W, C), 1.0, 6.0, ((0, 8), (1, 4)), jnp.float32)
    timesteps = touch_ends(jax.random.randint(keys[3], (STEPS,), 0, 1000), jax.random.fold_in(keys[3], 1), 0, 999).astype(jnp.int32)
    gain_space = jnp.clip(1.0 + 0.18 * jax.random.normal(keys[4], (C,), jnp.float32), 0.1, 1.9)
    gain_attention = jnp.clip(1.0 + 0.18 * jax.random.normal(keys[5], (C,), jnp.float32), 0.1, 1.9)
    time_weight = noise(keys[6], (C, 2 * C), C ** -0.5, 0.5, (), jnp.float32)
    space_weight = noise(keys[7], (9 * C, C), (9 * C) ** -0.5, 0.1875)
    attention_weight = draw_attention_weight(jax.random.fold_in(keys[10], 71), 0)
    output_weight = noise(keys[9], (C, C), C ** -0.5, 0.5)
    return {"start_state": start_state, "initial_guess": initial_guess, "noise_draws": noise_draws, "timesteps": timesteps, "gain_space": gain_space, "gain_attention": gain_attention, "time_weight": time_weight, "space_weight": space_weight, "attention_weight": attention_weight, "output_weight": output_weight}


def embed_time(step_value):
    half_width = C // 2
    frequency = jnp.exp(-math.log(10000.0) * jnp.arange(half_width, dtype=jnp.float32) / half_width)
    angles = step_value.astype(jnp.float32) * frequency
    return jnp.concatenate([jnp.cos(angles), jnp.sin(angles)])

def modulation(step_value, time_weight):
    encoded = embed_time(step_value)[None, :]
    shifted = jnp.dot(encoded, time_weight, precision=lax.Precision.HIGHEST, preferred_element_type=jnp.float32)[0]
    return (1.0 + shifted[:C], shifted[C:])

def normalize(field, gain):
    return field * lax.rsqrt(lax.optimization_barrier(jnp.mean(field * field, axis=-1, keepdims=True)) + 1e-06) * gain

def conv_taps(padded, space_weight):
    frames_here = padded.shape[0]
    rows_here = padded.shape[1] - 2
    cols_here = padded.shape[2] - 2
    shifted = [padded[:, row_shift:row_shift + rows_here, col_shift:col_shift + cols_here, :] for row_shift in range(3) for col_shift in range(3)]
    stacked = jnp.concatenate(shifted, axis=-1).reshape(-1, 9 * padded.shape[3])
    result = jnp.dot(stacked, space_weight, preferred_element_type=jnp.float32)
    return result.reshape(frames_here, rows_here, cols_here, space_weight.shape[1])

def attend(normed_in, attention_weight):
    frames_all, rows_here, cols_here, channels = normed_in.shape
    projected = jnp.dot(normed_in.reshape(-1, channels), attention_weight, preferred_element_type=jnp.float32).astype(jnp.bfloat16)
    projected = lax.optimization_barrier(projected).astype(jnp.float32)
    projected = projected.reshape(frames_all, rows_here, cols_here, 3, channels // HEAD_DIM, HEAD_DIM)
    query_vectors = projected[:, :, :, 0]
    key_vectors = projected[:, :, :, 1]
    value_vectors = projected[:, :, :, 2]
    scores = jnp.einsum('fxyhd,gxyhd->xyhfg', query_vectors, key_vectors) / math.sqrt(HEAD_DIM)
    weights = jax.nn.softmax(scores, axis=-1).astype(jnp.bfloat16)
    weights = lax.optimization_barrier(weights).astype(jnp.float32)
    attended = jnp.einsum('xyhfg,gxyhd->fxyhd', weights, value_vectors)
    return attended.reshape(frames_all, rows_here, cols_here, channels).astype(jnp.bfloat16)

def drift(state, step_value, gain_space, gain_attention, time_weight, space_weight, attention_weight, output_weight):
    scaling, offset = modulation(step_value, time_weight)
    normed = (normalize(state, gain_space) * scaling + offset).astype(jnp.bfloat16)
    padded = jnp.pad(normed, ((0, 0), (1, 1), (1, 1), (0, 0)))
    mixed_state = state + jax.nn.silu(conv_taps(padded, space_weight))
    attn_in = normalize(mixed_state, gain_attention).astype(jnp.bfloat16)
    attended = attend(attn_in, attention_weight)
    projected = jnp.dot(attended.reshape(-1, attended.shape[-1]), output_weight, preferred_element_type=jnp.float32)
    return mixed_state + projected.reshape(mixed_state.shape)

def reference(start_state, initial_guess, noise_draws, timesteps, gain_space, gain_attention, time_weight, space_weight, attention_weight, output_weight):
    steps_total = timesteps.shape[0]
    time_values = timesteps.astype(jnp.float32) / 1000.0
    coefficient = (0.5 + time_values) / math.sqrt(steps_total)

    def one_term(carried):
        state, noise_block, step_value, time_value, coeff_value = carried
        evaluated = drift(state, step_value, gain_space, gain_attention, time_weight, space_weight, attention_weight, output_weight)
        return coeff_value * (evaluated + time_value * noise_block)
    iterate = initial_guess
    before = jnp.zeros_like(initial_guess)
    terms = jnp.zeros_like(initial_guess)
    for picard_turn in range(ITERS):
        terms = lax.map(one_term, (iterate, noise_draws, timesteps, time_values, coefficient))
        before = jnp.cumsum(terms, axis=0) - terms
        iterate = start_state[None] + before
    return start_state[None] + (before + terms)
```

```python
import functools
import math

import jax
import jax.numpy as jnp
from jax import lax
from jax.experimental import pallas as pl
from jax.experimental.pallas import tpu as pltpu
from jax.sharding import PartitionSpec as P

HEAD_DIM = 64
ITERS = 2
PIECES = 4
EPS = 1e-06


def modulation(step_value, time_weight):
    channels = time_weight.shape[0]
    half_width = channels // 2
    frequency = jnp.exp(-math.log(10000.0) * jnp.arange(half_width, dtype=jnp.float32) / half_width)
    angles = step_value.astype(jnp.float32) * frequency
    encoded = jnp.concatenate([jnp.cos(angles), jnp.sin(angles)])[None, :]
    shifted = jnp.dot(
        encoded, time_weight, precision=lax.Precision.HIGHEST, preferred_element_type=jnp.float32
    )[0]
    return (1.0 + shifted[:channels], shifted[channels:])


def kernel(
    n_tm,
    n_frame,
    width,
    start_ref,
    guess_ref,
    noise_ref,
    rows_ref,
    wconv_ref,
    wattn_ref,
    wout_ref,
    out_ref,
    state,
    taps,
    mixed,
    term,
    proj,
    ain,
    rin,
    aout,
    rout,
    zin,
    zout,
    xin,
    in_send,
    in_recv,
    out_send,
    out_recv,
    z_send,
    z_recv,
    x_send,
    x_recv,
):
    cells, channels = start_ref.shape
    share = cells // n_frame
    piece = cells // PIECES
    me_tm = lax.axis_index("tm")
    me = lax.axis_index("frame")
    link = me_tm // 2
    side = lax.rem(me_tm, 2)
    links = n_tm // 2
    has_prev = link > 0
    has_next = link < links - 1

    def at_frame(f):
        return {"tm": me_tm, "frame": f}

    def at_tm(t):
        return {"tm": t, "frame": me}

    def peer(s):
        return lax.rem(me + s, n_frame)

    barrier = pltpu.get_barrier_semaphore()

    def greet(device):
        pl.semaphore_signal(barrier, inc=1, device_id=device, device_id_type=pl.DeviceIdType.MESH)

    for s in range(1, n_frame):
        greet(at_frame(peer(s)))
    greet(at_tm(me_tm + 1 - 2 * side))

    @pl.when(has_prev)
    def _():
        greet(at_tm(me_tm - 2))

    @pl.when(has_next)
    def _():
        greet(at_tm(me_tm + 2))

    def meet():
        pl.semaphore_wait(barrier, n_frame + has_prev.astype(jnp.int32) + has_next.astype(jnp.int32))

    edge = jnp.zeros((width, 3 * channels), jnp.bfloat16)
    taps[0:width, :] = edge
    taps[cells + width : cells + 2 * width, :] = edge

    @pl.when(link == 0)
    def _():
        zin[...] = jnp.zeros_like(zin)

    gain_space = rows_ref[0:1, :]
    offset = rows_ref[1:2, :]
    coefficient = rows_ref[2:3, :]
    time_value = rows_ref[3:4, :]
    gain_attention = rows_ref[4:5, :]

    def inverse_rms(v):
        return lax.rsqrt(jnp.mean(v * v, axis=-1, keepdims=True) + EPS)

    column = lax.broadcasted_iota(jnp.int32, (piece, channels), 0) % width
    head_in = lax.broadcasted_iota(jnp.int32, (2 * channels, channels), 0) % channels // HEAD_DIM
    head_to = lax.broadcasted_iota(jnp.int32, (2 * channels, channels), 1) // HEAD_DIM
    gather_heads = jnp.where(head_in == head_to, 1.0, 0.0).astype(jnp.bfloat16)

    for turn in range(ITERS):
        source = guess_ref if turn == 0 else state

        def make_taps(c, _):
            at = pl.multiple_of(c * piece, piece)
            x = source[pl.ds(at, piece), :]
            normed = x * inverse_rms(x) * gain_space + offset
            left = jnp.where(column == 0, 0.0, pltpu.roll(normed, 1, 0))
            right = jnp.where(column == width - 1, 0.0, pltpu.roll(normed, piece - 1, 0))
            to = pl.multiple_of(at + width, width)
            taps[pl.ds(to, piece), 0:channels] = left.astype(jnp.bfloat16)
            taps[pl.ds(to, piece), channels : 2 * channels] = normed.astype(jnp.bfloat16)
            taps[pl.ds(to, piece), 2 * channels : 3 * channels] = right.astype(jnp.bfloat16)
            return 0

        lax.fori_loop(0, PIECES, make_taps, 0)
        if turn == 0:
            meet()

        def in_copy(s):
            return pltpu.make_async_remote_copy(
                src_ref=ain.at[turn, peer(s)],
                dst_ref=rin.at[turn, me],
                send_sem=in_send.at[turn, s],
                recv_sem=in_recv.at[turn, s],
                device_id=at_frame(peer(s)),
                device_id_type=pl.DeviceIdType.MESH,
            )

        def mix(q):
            at = pl.multiple_of(q * share, share)
            total = jnp.zeros((share, channels), jnp.float32)
            for row in range(3):
                start = pl.multiple_of(at + row * width, width)
                total += jnp.dot(
                    taps[pl.ds(start, share), :],
                    wconv_ref[row * 3 * channels : (row + 1) * 3 * channels, :],
                    preferred_element_type=jnp.float32,
                )
            value = source[pl.ds(at, share), :] + total / (1.0 + jnp.exp(-total))
            mixed[pl.ds(at, share), :] = value
            return (value * inverse_rms(value) * gain_attention).astype(jnp.bfloat16)

        def mix_and_send(s, _):
            q = peer(s)
            ain[turn, q] = mix(q)
            in_copy(s).start()
            return 0

        lax.fori_loop(1, n_frame, mix_and_send, 0)
        rin[turn, me] = mix(me)

        def project(f):
            proj[f] = (
                jnp.dot(rin[turn, f], wattn_ref[...], preferred_element_type=jnp.float32)
                .astype(jnp.bfloat16)
                .astype(jnp.float32)
            )

        project(me)

        def arrive(s, _):
            in_copy(s).wait()
            project(lax.rem(me + n_frame - s, n_frame))
            return 0

        lax.fori_loop(1, n_frame, arrive, 0)

        def attend(f):
            query = proj[f, :, 0:channels]
            products = (query[None] * proj[:, :, channels : 2 * channels]).reshape(-1, channels)
            high = products.astype(jnp.bfloat16)
            low = (products - high.astype(jnp.float32)).astype(jnp.bfloat16)
            scores = jnp.dot(
                jnp.concatenate([high, low], axis=-1), gather_heads, preferred_element_type=jnp.float32
            ).reshape(n_frame, share, channels) * (1.0 / math.sqrt(HEAD_DIM))
            raised = jnp.exp(scores - jnp.max(scores, axis=0, keepdims=True))
            weights = raised / jnp.sum(raised, axis=0, keepdims=True)
            weights = weights.astype(jnp.bfloat16).astype(jnp.float32)
            return jnp.sum(weights * proj[:, :, 2 * channels : 3 * channels], axis=0).astype(jnp.bfloat16)

        def out_copy(s):
            return pltpu.make_async_remote_copy(
                src_ref=aout.at[turn, peer(s)],
                dst_ref=rout.at[turn, me],
                send_sem=out_send.at[turn, s],
                recv_sem=out_recv.at[turn, s],
                device_id=at_frame(peer(s)),
                device_id_type=pl.DeviceIdType.MESH,
            )

        def attend_and_send(s, _):
            f = peer(s)
            aout[turn, f] = attend(f)
            out_copy(s).start()
            return 0

        lax.fori_loop(1, n_frame, attend_and_send, 0)
        rout[turn, me] = attend(me)

        def close(q):
            at = pl.multiple_of(q * share, share)
            drift = mixed[pl.ds(at, share), :] + jnp.dot(
                rout[turn, q], wout_ref[...], preferred_element_type=jnp.float32
            )
            term[pl.ds(at, share), :] = coefficient * (drift + time_value * noise_ref[pl.ds(at, share), :])

        close(me)

        def land(s, _):
            out_copy(s).wait()
            close(lax.rem(me + n_frame - s, n_frame))
            return 0

        lax.fori_loop(1, n_frame, land, 0)

        def z_copy(c):
            return pltpu.make_async_remote_copy(
                src_ref=zout.at[turn, c],
                dst_ref=zin.at[turn, c],
                send_sem=z_send.at[turn, c],
                recv_sem=z_recv.at[turn, c],
                device_id=at_tm(me_tm + 2),
                device_id_type=pl.DeviceIdType.MESH,
            )

        def x_copy(c, src):
            return pltpu.make_async_remote_copy(
                src_ref=src.at[turn, c],
                dst_ref=xin.at[turn, c],
                send_sem=x_send.at[turn, c],
                recv_sem=x_recv.at[turn, c],
                device_id=at_tm(me_tm + 1 - 2 * side),
                device_id_type=pl.DeviceIdType.MESH,
            )

        def chain(c, _):
            at = pl.multiple_of(c * piece, piece)

            @pl.when(has_prev)
            def _():
                z_copy(c).wait_recv()

            zout[turn, c] = zin[turn, c] + term[pl.ds(at, piece), :]

            @pl.when(has_next)
            def _():
                z_copy(c).start()

            @pl.when(side == 0)
            def _():
                x_copy(c, zout).start()

            @pl.when(side == 1)
            def _():
                x_copy(c, zin).start()

            return 0

        lax.fori_loop(0, PIECES, chain, 0)

        def finish(c, _):
            at = pl.multiple_of(c * piece, piece)
            x_copy(c, zout).wait()
            before = zin[turn, c] + xin[turn, c]
            if turn == ITERS - 1:
                out_ref[pl.ds(at, piece), :] = before + term[pl.ds(at, piece), :]
            else:
                state[pl.ds(at, piece), :] = start_ref[pl.ds(at, piece), :] + before

            @pl.when(has_next)
            def _():
                z_copy(c).wait_send()

            return 0

        lax.fori_loop(0, PIECES, finish, 0)


def shards(
    n_tm,
    n_frame,
    start_state,
    initial_guess,
    noise_draws,
    timesteps,
    gain_space,
    gain_attention,
    time_weight,
    space_weight,
    attention_weight,
    output_weight,
):
    _, height, width, channels = start_state.shape
    cells = height * width
    share = cells // n_frame
    piece = cells // PIECES
    step_value = timesteps[0]
    time_value = step_value.astype(jnp.float32) / 1000.0
    coefficient = (0.5 + time_value) / math.sqrt(n_tm)
    scaling, offset = modulation(step_value, time_weight)
    rows = jnp.stack(
        [
            gain_space * scaling,
            offset,
            jnp.full((channels,), coefficient),
            jnp.full((channels,), time_value),
            gain_attention,
        ]
    )
    vmem = pl.BlockSpec(memory_space=pltpu.VMEM)
    f32, bf16 = jnp.float32, jnp.bfloat16
    dma = pltpu.SemaphoreType.DMA
    exchange = pltpu.VMEM((ITERS, n_frame, share, channels), bf16)
    sums = pltpu.VMEM((ITERS, PIECES, piece, channels), f32)
    total = pl.pallas_call(
        functools.partial(kernel, n_tm, n_frame, width),
        out_shape=jax.ShapeDtypeStruct((cells, channels), f32),
        in_specs=[vmem] * 7,
        out_specs=vmem,
        scratch_shapes=[
            pltpu.VMEM((cells, channels), f32),
            pltpu.VMEM((cells + 2 * width, 3 * channels), bf16),
            pltpu.VMEM((cells, channels), f32),
            pltpu.VMEM((cells, channels), f32),
            pltpu.VMEM((n_frame, share, 3 * channels), f32),
            exchange,
            exchange,
            exchange,
            exchange,
            sums,
            sums,
            sums,
            dma((ITERS, n_frame)),
            dma((ITERS, n_frame)),
            dma((ITERS, n_frame)),
            dma((ITERS, n_frame)),
            dma((ITERS, PIECES)),
            dma((ITERS, PIECES)),
            dma((ITERS, PIECES)),
            dma((ITERS, PIECES)),
        ],
        compiler_params=pltpu.CompilerParams(collective_id=0, has_side_effects=True),
    )(
        start_state.reshape(cells, channels),
        initial_guess.reshape(cells, channels),
        noise_draws.reshape(cells, channels),
        rows,
        space_weight,
        attention_weight,
        output_weight,
    )
    return start_state[None] + total.reshape(1, 1, height, width, channels)


def solution(mesh):
    return jax.shard_map(
        functools.partial(shards, mesh.shape["tm"], mesh.shape["frame"]),
        mesh=mesh,
        in_specs=(
            P("frame", None, None, None),
            P("tm", "frame", None, None, None),
            P("tm", "frame", None, None, None),
            P("tm"),
            P(),
            P(),
            P(),
            P(),
            P(),
            P(),
        ),
        out_specs=P("tm", "frame", None, None, None),
        check_vma=False,
    )
```

```python
import functools
import math

import jax
import jax.numpy as jnp
from jax import lax
from jax.experimental import pallas as pl
from jax.experimental.pallas import tpu as pltpu
from jax.sharding import PartitionSpec as P

HEAD_DIM = 64
ITERS = 2
GROUPS = 2
X_TYPE = jnp.bfloat16
Z_TYPE = jnp.float32
EPS = 1e-06


def modulation(step_value, time_weight):
    channels = time_weight.shape[0]
    half_width = channels // 2
    frequency = jnp.exp(-math.log(10000.0) * jnp.arange(half_width, dtype=jnp.float32) / half_width)
    angles = step_value.astype(jnp.float32) * frequency
    encoded = jnp.concatenate([jnp.cos(angles), jnp.sin(angles)])[None, :]
    shifted = jnp.dot(
        encoded, time_weight, precision=lax.Precision.HIGHEST, preferred_element_type=jnp.float32
    )[0]
    return (1.0 + shifted[:channels], shifted[channels:])


def kernel(
    n_tm,
    n_frame,
    width,
    groups,
    start_ref,
    guess_ref,
    noise_ref,
    rows_ref,
    wconv_ref,
    wattn_ref,
    wout_ref,
    out_ref,
    state,
    taps,
    mixed,
    term,
    proj,
    ain,
    rin,
    aout,
    rout,
    pair_out,
    pair_in,
    zout,
    zin,
    back_out,
    back_in,
    in_send,
    in_recv,
    out_send,
    out_recv,
    pair_send,
    pair_recv,
    z_send,
    z_recv,
    back_send,
    back_recv,
):
    cells, channels = start_ref.shape
    share = cells // n_frame
    piece = share // groups
    half = piece // 2
    pieces = n_frame * groups
    me_tm = lax.axis_index("tm")
    me = lax.axis_index("frame")
    link = me_tm // 2
    side = lax.rem(me_tm, 2)
    links = n_tm // 2
    has_prev = link > 0
    has_next = link < links - 1

    def at_frame(f):
        return {"tm": me_tm, "frame": f}

    def at_tm(t):
        return {"tm": t, "frame": me}

    def peer(s):
        return lax.rem(me + s, n_frame)

    def sender(s):
        return lax.rem(me + n_frame - s, n_frame)

    barrier = pltpu.get_barrier_semaphore()

    def greet(device):
        pl.semaphore_signal(barrier, inc=1, device_id=device, device_id_type=pl.DeviceIdType.MESH)

    for s in range(1, n_frame):
        greet(at_frame(peer(s)))
    greet(at_tm(me_tm + 1 - 2 * side))

    @pl.when(has_prev)
    def _():
        greet(at_tm(me_tm - 2))

    @pl.when(has_next)
    def _():
        greet(at_tm(me_tm + 2))

    def meet():
        pl.semaphore_wait(barrier, n_frame + has_prev.astype(jnp.int32) + has_next.astype(jnp.int32))

    edge = jnp.zeros((width, 3 * channels), jnp.bfloat16)
    taps[0:width, :] = edge
    taps[cells + width : cells + 2 * width, :] = edge

    @pl.when(link == 0)
    def _():
        zin[...] = jnp.zeros_like(zin)

    gain_space = rows_ref[0:1, :]
    offset = rows_ref[1:2, :]
    coefficient = rows_ref[2:3, :]
    time_value = rows_ref[3:4, :]
    gain_attention = rows_ref[4:5, :]

    def inverse_rms(v):
        return lax.rsqrt(jnp.mean(v * v, axis=-1, keepdims=True) + EPS)

    column = lax.broadcasted_iota(jnp.int32, (piece, channels), 0) % width
    head_in = lax.broadcasted_iota(jnp.int32, (2 * channels, channels), 0) % channels // HEAD_DIM
    head_to = lax.broadcasted_iota(jnp.int32, (2 * channels, channels), 1) // HEAD_DIM
    gather_heads = jnp.where(head_in == head_to, 1.0, 0.0).astype(jnp.bfloat16)

    def make_taps(at, x):
        normed = x * inverse_rms(x) * gain_space + offset
        left = jnp.where(column == 0, 0.0, pltpu.roll(normed, 1, 0))
        right = jnp.where(column == width - 1, 0.0, pltpu.roll(normed, piece - 1, 0))
        to = pl.multiple_of(at + width, width)
        taps[pl.ds(to, piece), 0:channels] = left.astype(jnp.bfloat16)
        taps[pl.ds(to, piece), channels : 2 * channels] = normed.astype(jnp.bfloat16)
        taps[pl.ds(to, piece), 2 * channels : 3 * channels] = right.astype(jnp.bfloat16)

    def first_taps(i, _):
        at = pl.multiple_of(i * piece, piece)
        make_taps(at, guess_ref[pl.ds(at, piece), :])
        return 0

    def remote(src, dst, send, recv, device):
        return pltpu.make_async_remote_copy(
            src_ref=src,
            dst_ref=dst,
            send_sem=send,
            recv_sem=recv,
            device_id=device,
            device_id_type=pl.DeviceIdType.MESH,
        )

    for turn in range(ITERS):
        source = guess_ref if turn == 0 else state
        if turn == 0:
            lax.fori_loop(0, pieces, first_taps, 0)
            meet()

        def in_copy(s, g):
            return remote(
                ain.at[turn, g, peer(s)],
                rin.at[turn, g, me],
                in_send.at[turn, g, s],
                in_recv.at[turn, g, s],
                at_frame(peer(s)),
            )

        def out_copy(s, g):
            return remote(
                aout.at[turn, g, peer(s)],
                rout.at[turn, g, me],
                out_send.at[turn, g, s],
                out_recv.at[turn, g, s],
                at_frame(peer(s)),
            )

        def pair_copy(i):
            return remote(
                pair_out.at[turn, i],
                pair_in.at[turn, i],
                pair_send.at[turn, i],
                pair_recv.at[turn, i],
                at_tm(me_tm + 1 - 2 * side),
            )

        def z_copy(i):
            return remote(
                zout.at[turn, i], zin.at[turn, i], z_send.at[turn, i], z_recv.at[turn, i], at_tm(me_tm + 2)
            )

        def back_copy(i):
            return remote(
                back_out.at[turn, i],
                back_in.at[turn, i],
                back_send.at[turn, i],
                back_recv.at[turn, i],
                at_tm(me_tm + 1 - 2 * side),
            )

        def mix(q, g):
            at = pl.multiple_of(q * share + g * piece, piece)
            total = jnp.zeros((piece, channels), jnp.float32)
            for row in range(3):
                start = pl.multiple_of(at + row * width, width)
                total += jnp.dot(
                    taps[pl.ds(start, piece), :],
                    wconv_ref[row * 3 * channels : (row + 1) * 3 * channels, :],
                    preferred_element_type=jnp.float32,
                )
            value = source[pl.ds(at, piece), :] + total / (1.0 + jnp.exp(-total))
            mixed[pl.ds(at, piece), :] = value
            return (value * inverse_rms(value) * gain_attention).astype(jnp.bfloat16)

        def project(f, g):
            proj[g, f] = (
                jnp.dot(rin[turn, g, f], wattn_ref[...], preferred_element_type=jnp.float32)
                .astype(jnp.bfloat16)
                .astype(jnp.float32)
            )

        def attend(f, g):
            query = proj[g, f, :, 0:channels]
            products = (query[None] * proj[g, :, :, channels : 2 * channels]).reshape(-1, channels)
            high = products.astype(jnp.bfloat16)
            low = (products - high.astype(jnp.float32)).astype(jnp.bfloat16)
            scores = jnp.dot(
                jnp.concatenate([high, low], axis=-1), gather_heads, preferred_element_type=jnp.float32
            ).reshape(n_frame, piece, channels) * (1.0 / math.sqrt(HEAD_DIM))
            raised = jnp.exp(scores - jnp.max(scores, axis=0, keepdims=True))
            weights = raised / jnp.sum(raised, axis=0, keepdims=True)
            weights = weights.astype(jnp.bfloat16).astype(jnp.float32)
            return jnp.sum(weights * proj[g, :, :, 2 * channels : 3 * channels], axis=0).astype(jnp.bfloat16)

        def place(i):
            return pl.multiple_of(sender(i % n_frame) * share + i // n_frame * piece, piece)

        for g in range(groups):

            def mix_and_send(s, _):
                q = peer(s)
                ain[turn, g, q] = mix(q, g)
                in_copy(s, g).start()
                return 0

            lax.fori_loop(1, n_frame, mix_and_send, 0)
            rin[turn, g, me] = mix(me, g)
            project(me, g)

        for g in range(groups):

            def arrive(s, _):
                in_copy(s, g).wait_recv()
                project(sender(s), g)
                return 0

            lax.fori_loop(1, n_frame, arrive, 0)

            def attend_and_send(s, _):
                f = peer(s)
                aout[turn, g, f] = attend(f, g)
                out_copy(s, g).start()
                return 0

            lax.fori_loop(1, n_frame, attend_and_send, 0)
            rout[turn, g, me] = attend(me, g)

        for g in range(groups):

            def close(s):
                q = sender(s)
                i = g * n_frame + s
                at = pl.multiple_of(q * share + g * piece, piece)
                drift = mixed[pl.ds(at, piece), :] + jnp.dot(
                    rout[turn, g, q], wout_ref[...], preferred_element_type=jnp.float32
                )
                term[pl.ds(at, piece), :] = coefficient * (drift + time_value * noise_ref[pl.ds(at, piece), :])
                other = pl.multiple_of(at + (1 - side) * half, half)
                pair_out[turn, i] = term[pl.ds(other, half), :].astype(pair_out.dtype)
                pair_copy(i).start()

            close(0)

            def land(s, _):
                out_copy(s, g).wait_recv()
                close(s)
                return 0

            lax.fori_loop(1, n_frame, land, 0)

        def chain(i, _):
            own = pl.multiple_of(place(i) + side * half, half)
            mine = term[pl.ds(own, half), :]
            pair_copy(i).wait_recv()
            both = mine + pair_in[turn, i].astype(jnp.float32)

            @pl.when(has_prev)
            def _():
                z_copy(i).wait_recv()

            earlier = zin[turn, i].astype(jnp.float32)

            @pl.when(has_next)
            def _():
                zout[turn, i] = (earlier + both).astype(zout.dtype)
                z_copy(i).start()

            back_out[turn, i] = jnp.where(side == 0, earlier + mine, earlier).astype(back_out.dtype)
            back_copy(i).start()
            return 0

        lax.fori_loop(0, pieces, chain, 0)

        def finish(i, _):
            at = place(i)
            own = pl.multiple_of(at + side * half, half)
            other = pl.multiple_of(at + (1 - side) * half, half)
            last = turn == ITERS - 1
            base, target = (term, out_ref) if last else (start_ref, state)
            earlier = zin[turn, i].astype(jnp.float32)
            first = jnp.where(side == 0, earlier, earlier + pair_in[turn, i].astype(jnp.float32))
            target[pl.ds(own, half), :] = base[pl.ds(own, half), :] + first
            back_copy(i).wait_recv()
            target[pl.ds(other, half), :] = base[pl.ds(other, half), :] + back_in[turn, i].astype(jnp.float32)
            if not last:
                make_taps(at, state[pl.ds(at, piece), :])
            return 0

        lax.fori_loop(0, pieces, finish, 0)

        def sent(i, _):
            pair_copy(i).wait_send()
            back_copy(i).wait_send()

            @pl.when(has_next)
            def _():
                z_copy(i).wait_send()

            return 0

        lax.fori_loop(0, pieces, sent, 0)

        for g in range(groups):

            def left(s, _):
                in_copy(s, g).wait_send()
                out_copy(s, g).wait_send()
                return 0

            lax.fori_loop(1, n_frame, left, 0)


def shards(
    n_tm,
    n_frame,
    start_state,
    initial_guess,
    noise_draws,
    timesteps,
    gain_space,
    gain_attention,
    time_weight,
    space_weight,
    attention_weight,
    output_weight,
):
    _, height, width, channels = start_state.shape
    cells = height * width
    share = cells // n_frame
    groups = GROUPS if share // width % GROUPS == 0 else 1
    piece = share // groups
    pieces = n_frame * groups
    step_value = timesteps[0]
    time_value = step_value.astype(jnp.float32) / 1000.0
    coefficient = (0.5 + time_value) / math.sqrt(n_tm)
    scaling, offset = modulation(step_value, time_weight)
    rows = jnp.stack(
        [
            gain_space * scaling,
            offset,
            jnp.full((channels,), coefficient),
            jnp.full((channels,), time_value),
            gain_attention,
        ]
    )
    vmem = pl.BlockSpec(memory_space=pltpu.VMEM)
    f32, bf16 = jnp.float32, jnp.bfloat16
    dma = pltpu.SemaphoreType.DMA
    exchange = pltpu.VMEM((ITERS, groups, n_frame, piece, channels), bf16)
    cross = pltpu.VMEM((ITERS, pieces, piece // 2, channels), X_TYPE)
    along = pltpu.VMEM((ITERS, pieces, piece // 2, channels), Z_TYPE)
    total = pl.pallas_call(
        functools.partial(kernel, n_tm, n_frame, width, groups),
        out_shape=jax.ShapeDtypeStruct((cells, channels), f32),
        in_specs=[vmem] * 7,
        out_specs=vmem,
        scratch_shapes=[
            pltpu.VMEM((cells, channels), f32),
            pltpu.VMEM((cells + 2 * width, 3 * channels), bf16),
            pltpu.VMEM((cells, channels), f32),
            pltpu.VMEM((cells, channels), f32),
            pltpu.VMEM((groups, n_frame, piece, 3 * channels), f32),
            exchange,
            exchange,
            exchange,
            exchange,
            cross,
            cross,
            along,
            along,
            cross,
            cross,
            *([dma((ITERS, groups, n_frame))] * 4),
            *([dma((ITERS, pieces))] * 6),
        ],
        compiler_params=pltpu.CompilerParams(collective_id=0, has_side_effects=True),
    )(
        start_state.reshape(cells, channels),
        initial_guess.reshape(cells, channels),
        noise_draws.reshape(cells, channels),
        rows,
        space_weight,
        attention_weight,
        output_weight,
    )
    return start_state[None] + total.reshape(1, 1, height, width, channels)


def solution(mesh):
    return jax.shard_map(
        functools.partial(shards, mesh.shape["tm"], mesh.shape["frame"]),
        mesh=mesh,
        in_specs=(
            P("frame", None, None, None),
            P("tm", "frame", None, None, None),
            P("tm", "frame", None, None, None),
            P("tm"),
            P(),
            P(),
            P(),
            P(),
            P(),
            P(),
        ),
        out_specs=P("tm", "frame", None, None, None),
        check_vma=False,
    )
```

```python
import functools
import math

import jax
import jax.numpy as jnp
from jax import lax
from jax.experimental import pallas as pl
from jax.experimental.pallas import tpu as pltpu
from jax.sharding import PartitionSpec as P

HEAD_DIM = 64
ITERS = 2
GROUPS = 2
X_TYPE = jnp.bfloat16
Z_TYPES = (jnp.bfloat16, jnp.float32)
EPS = 1e-06


def modulation(step_value, time_weight):
    channels = time_weight.shape[0]
    half_width = channels // 2
    frequency = jnp.exp(-math.log(10000.0) * jnp.arange(half_width, dtype=jnp.float32) / half_width)
    angles = step_value.astype(jnp.float32) * frequency
    encoded = jnp.concatenate([jnp.cos(angles), jnp.sin(angles)])[None, :]
    shifted = jnp.dot(
        encoded, time_weight, precision=lax.Precision.HIGHEST, preferred_element_type=jnp.float32
    )[0]
    return (1.0 + shifted[:channels], shifted[channels:])


def kernel(
    n_tm,
    n_frame,
    width,
    groups,
    start_ref,
    guess_ref,
    noise_ref,
    rows_ref,
    wconv_ref,
    wattn_ref,
    wout_ref,
    out_ref,
    state,
    taps,
    mixed,
    term,
    proj,
    ain,
    rin,
    aout,
    rout,
    pair_out,
    pair_in,
    zout_first,
    zout_last,
    zin_first,
    zin_last,
    back_out,
    back_in,
    in_send,
    in_recv,
    out_send,
    out_recv,
    pair_send,
    pair_recv,
    z_send,
    z_recv,
    back_send,
    back_recv,
):
    cells, channels = start_ref.shape
    share = cells // n_frame
    piece = share // groups
    half = piece // 2
    pieces = n_frame * groups
    me_tm = lax.axis_index("tm")
    me = lax.axis_index("frame")
    link = me_tm // 2
    side = lax.rem(me_tm, 2)
    links = n_tm // 2
    has_prev = link > 0
    has_next = link < links - 1

    def at_frame(f):
        return {"tm": me_tm, "frame": f}

    def at_tm(t):
        return {"tm": t, "frame": me}

    def peer(s):
        return lax.rem(me + s, n_frame)

    def sender(s):
        return lax.rem(me + n_frame - s, n_frame)

    barrier = pltpu.get_barrier_semaphore()

    def greet(device):
        pl.semaphore_signal(barrier, inc=1, device_id=device, device_id_type=pl.DeviceIdType.MESH)

    for s in range(1, n_frame):
        greet(at_frame(peer(s)))
    greet(at_tm(me_tm + 1 - 2 * side))

    @pl.when(has_prev)
    def _():
        greet(at_tm(me_tm - 2))

    @pl.when(has_next)
    def _():
        greet(at_tm(me_tm + 2))

    def meet():
        pl.semaphore_wait(barrier, n_frame + has_prev.astype(jnp.int32) + has_next.astype(jnp.int32))

    edge = jnp.zeros((width, 3 * channels), jnp.bfloat16)
    taps[0:width, :] = edge
    taps[cells + width : cells + 2 * width, :] = edge

    @pl.when(link == 0)
    def _():
        zin_first[...] = jnp.zeros_like(zin_first)
        zin_last[...] = jnp.zeros_like(zin_last)

    gain_space = rows_ref[0:1, :]
    offset = rows_ref[1:2, :]
    coefficient = rows_ref[2:3, :]
    time_value = rows_ref[3:4, :]
    gain_attention = rows_ref[4:5, :]

    def inverse_rms(v):
        return lax.rsqrt(jnp.mean(v * v, axis=-1, keepdims=True) + EPS)

    column = lax.broadcasted_iota(jnp.int32, (piece, channels), 0) % width
    head_in = lax.broadcasted_iota(jnp.int32, (2 * channels, channels), 0) % channels // HEAD_DIM
    head_to = lax.broadcasted_iota(jnp.int32, (2 * channels, channels), 1) // HEAD_DIM
    gather_heads = jnp.where(head_in == head_to, 1.0, 0.0).astype(jnp.bfloat16)

    def make_taps(at, x):
        normed = x * inverse_rms(x) * gain_space + offset
        left = jnp.where(column == 0, 0.0, pltpu.roll(normed, 1, 0))
        right = jnp.where(column == width - 1, 0.0, pltpu.roll(normed, piece - 1, 0))
        to = pl.multiple_of(at + width, width)
        taps[pl.ds(to, piece), 0:channels] = left.astype(jnp.bfloat16)
        taps[pl.ds(to, piece), channels : 2 * channels] = normed.astype(jnp.bfloat16)
        taps[pl.ds(to, piece), 2 * channels : 3 * channels] = right.astype(jnp.bfloat16)

    def first_taps(i, _):
        at = pl.multiple_of(i * piece, piece)
        make_taps(at, guess_ref[pl.ds(at, piece), :])
        return 0

    def remote(src, dst, send, recv, device):
        return pltpu.make_async_remote_copy(
            src_ref=src,
            dst_ref=dst,
            send_sem=send,
            recv_sem=recv,
            device_id=device,
            device_id_type=pl.DeviceIdType.MESH,
        )

    for turn in range(ITERS):
        source = guess_ref if turn == 0 else state
        zout, zin = (zout_last, zin_last) if turn == ITERS - 1 else (zout_first, zin_first)
        if turn == 0:
            lax.fori_loop(0, pieces, first_taps, 0)
            meet()

        def in_copy(s, g):
            return remote(
                ain.at[turn, g, peer(s)],
                rin.at[turn, g, me],
                in_send.at[turn, g, s],
                in_recv.at[turn, g, s],
                at_frame(peer(s)),
            )

        def out_copy(s, g):
            return remote(
                aout.at[turn, g, peer(s)],
                rout.at[turn, g, me],
                out_send.at[turn, g, s],
                out_recv.at[turn, g, s],
                at_frame(peer(s)),
            )

        def pair_copy(i):
            return remote(
                pair_out.at[turn, i],
                pair_in.at[turn, i],
                pair_send.at[turn, i],
                pair_recv.at[turn, i],
                at_tm(me_tm + 1 - 2 * side),
            )

        def z_copy(i):
            return remote(
                zout.at[turn, i], zin.at[turn, i], z_send.at[turn, i], z_recv.at[turn, i], at_tm(me_tm + 2)
            )

        def back_copy(i):
            return remote(
                back_out.at[turn, i],
                back_in.at[turn, i],
                back_send.at[turn, i],
                back_recv.at[turn, i],
                at_tm(me_tm + 1 - 2 * side),
            )

        def mix(q, g):
            at = pl.multiple_of(q * share + g * piece, piece)
            total = jnp.zeros((piece, channels), jnp.float32)
            for row in range(3):
                start = pl.multiple_of(at + row * width, width)
                total += jnp.dot(
                    taps[pl.ds(start, piece), :],
                    wconv_ref[row * 3 * channels : (row + 1) * 3 * channels, :],
                    preferred_element_type=jnp.float32,
                )
            value = source[pl.ds(at, piece), :] + total / (1.0 + jnp.exp(-total))
            mixed[pl.ds(at, piece), :] = value
            return (value * inverse_rms(value) * gain_attention).astype(jnp.bfloat16)

        def project(f, g):
            proj[g, f] = (
                jnp.dot(rin[turn, g, f], wattn_ref[...], preferred_element_type=jnp.float32)
                .astype(jnp.bfloat16)
                .astype(jnp.float32)
            )

        def attend(f, g):
            query = proj[g, f, :, 0:channels]
            products = (query[None] * proj[g, :, :, channels : 2 * channels]).reshape(-1, channels)
            high = products.astype(jnp.bfloat16)
            low = (products - high.astype(jnp.float32)).astype(jnp.bfloat16)
            scores = jnp.dot(
                jnp.concatenate([high, low], axis=-1), gather_heads, preferred_element_type=jnp.float32
            ).reshape(n_frame, piece, channels) * (1.0 / math.sqrt(HEAD_DIM))
            raised = jnp.exp(scores - jnp.max(scores, axis=0, keepdims=True))
            weights = raised / jnp.sum(raised, axis=0, keepdims=True)
            weights = weights.astype(jnp.bfloat16).astype(jnp.float32)
            return jnp.sum(weights * proj[g, :, :, 2 * channels : 3 * channels], axis=0).astype(jnp.bfloat16)

        def place(i):
            return pl.multiple_of(sender(i % n_frame) * share + i // n_frame * piece, piece)

        for g in range(groups):

            def mix_and_send(s, _):
                q = peer(s)
                ain[turn, g, q] = mix(q, g)
                in_copy(s, g).start()
                return 0

            lax.fori_loop(1, n_frame, mix_and_send, 0)
            rin[turn, g, me] = mix(me, g)
            project(me, g)

        for g in range(groups):

            def arrive(s, _):
                in_copy(s, g).wait_recv()
                project(sender(s), g)
                return 0

            lax.fori_loop(1, n_frame, arrive, 0)

            def attend_and_send(s, _):
                f = peer(s)
                aout[turn, g, f] = attend(f, g)
                out_copy(s, g).start()
                return 0

            lax.fori_loop(1, n_frame, attend_and_send, 0)
            rout[turn, g, me] = attend(me, g)

        for g in range(groups):

            def close(s):
                q = sender(s)
                i = g * n_frame + s
                at = pl.multiple_of(q * share + g * piece, piece)
                drift = mixed[pl.ds(at, piece), :] + jnp.dot(
                    rout[turn, g, q], wout_ref[...], preferred_element_type=jnp.float32
                )
                term[pl.ds(at, piece), :] = coefficient * (drift + time_value * noise_ref[pl.ds(at, piece), :])
                other = pl.multiple_of(at + (1 - side) * half, half)
                pair_out[turn, i] = term[pl.ds(other, half), :].astype(pair_out.dtype)
                pair_copy(i).start()

            close(0)

            def land(s, _):
                out_copy(s, g).wait_recv()
                close(s)
                return 0

            lax.fori_loop(1, n_frame, land, 0)

        def chain(i, _):
            own = pl.multiple_of(place(i) + side * half, half)
            mine = term[pl.ds(own, half), :]
            pair_copy(i).wait_recv()
            both = mine + pair_in[turn, i].astype(jnp.float32)

            @pl.when(has_prev)
            def _():
                z_copy(i).wait_recv()

            earlier = zin[turn, i].astype(jnp.float32)

            @pl.when(has_next)
            def _():
                zout[turn, i] = (earlier + both).astype(zout.dtype)
                z_copy(i).start()

            back_out[turn, i] = jnp.where(side == 0, earlier + mine, earlier).astype(back_out.dtype)
            back_copy(i).start()
            return 0

        lax.fori_loop(0, pieces, chain, 0)

        def finish(i, _):
            at = place(i)
            own = pl.multiple_of(at + side * half, half)
            other = pl.multiple_of(at + (1 - side) * half, half)
            last = turn == ITERS - 1
            base, target = (term, out_ref) if last else (start_ref, state)
            earlier = zin[turn, i].astype(jnp.float32)
            first = jnp.where(side == 0, earlier, earlier + pair_in[turn, i].astype(jnp.float32))
            target[pl.ds(own, half), :] = base[pl.ds(own, half), :] + first
            back_copy(i).wait_recv()
            target[pl.ds(other, half), :] = base[pl.ds(other, half), :] + back_in[turn, i].astype(jnp.float32)
            if not last:
                make_taps(at, state[pl.ds(at, piece), :])
            return 0

        lax.fori_loop(0, pieces, finish, 0)

        def sent(i, _):
            pair_copy(i).wait_send()
            back_copy(i).wait_send()

            @pl.when(has_next)
            def _():
                z_copy(i).wait_send()

            return 0

        lax.fori_loop(0, pieces, sent, 0)

        for g in range(groups):

            def left(s, _):
                in_copy(s, g).wait_send()
                out_copy(s, g).wait_send()
                return 0

            lax.fori_loop(1, n_frame, left, 0)


def shards(
    n_tm,
    n_frame,
    start_state,
    initial_guess,
    noise_draws,
    timesteps,
    gain_space,
    gain_attention,
    time_weight,
    space_weight,
    attention_weight,
    output_weight,
):
    _, height, width, channels = start_state.shape
    cells = height * width
    share = cells // n_frame
    groups = GROUPS if share // width % GROUPS == 0 else 1
    piece = share // groups
    pieces = n_frame * groups
    step_value = timesteps[0]
    time_value = step_value.astype(jnp.float32) / 1000.0
    coefficient = (0.5 + time_value) / math.sqrt(n_tm)
    scaling, offset = modulation(step_value, time_weight)
    rows = jnp.stack(
        [
            gain_space * scaling,
            offset,
            jnp.full((channels,), coefficient),
            jnp.full((channels,), time_value),
            gain_attention,
        ]
    )
    vmem = pl.BlockSpec(memory_space=pltpu.VMEM)
    f32, bf16 = jnp.float32, jnp.bfloat16
    dma = pltpu.SemaphoreType.DMA
    exchange = pltpu.VMEM((ITERS, groups, n_frame, piece, channels), bf16)
    cross = pltpu.VMEM((ITERS, pieces, piece // 2, channels), X_TYPE)
    along = [pltpu.VMEM((ITERS, pieces, piece // 2, channels), kind) for kind in Z_TYPES]
    total = pl.pallas_call(
        functools.partial(kernel, n_tm, n_frame, width, groups),
        out_shape=jax.ShapeDtypeStruct((cells, channels), f32),
        in_specs=[vmem] * 7,
        out_specs=vmem,
        scratch_shapes=[
            pltpu.VMEM((cells, channels), f32),
            pltpu.VMEM((cells + 2 * width, 3 * channels), bf16),
            pltpu.VMEM((cells, channels), f32),
            pltpu.VMEM((cells, channels), f32),
            pltpu.VMEM((groups, n_frame, piece, 3 * channels), f32),
            exchange,
            exchange,
            exchange,
            exchange,
            cross,
            cross,
            *along,
            *along,
            cross,
            cross,
            *([dma((ITERS, groups, n_frame))] * 4),
            *([dma((ITERS, pieces))] * 6),
        ],
        compiler_params=pltpu.CompilerParams(collective_id=0, has_side_effects=True),
    )(
        start_state.reshape(cells, channels),
        initial_guess.reshape(cells, channels),
        noise_draws.reshape(cells, channels),
        rows,
        space_weight,
        attention_weight,
        output_weight,
    )
    return start_state[None] + total.reshape(1, 1, height, width, channels)


def solution(mesh):
    return jax.shard_map(
        functools.partial(shards, mesh.shape["tm"], mesh.shape["frame"]),
        mesh=mesh,
        in_specs=(
            P("frame", None, None, None),
            P("tm", "frame", None, None, None),
            P("tm", "frame", None, None, None),
            P("tm"),
            P(),
            P(),
            P(),
            P(),
            P(),
            P(),
        ),
        out_specs=P("tm", "frame", None, None, None),
        check_vma=False,
    )
```

```python
import functools
import math

import jax
import jax.numpy as jnp
from jax import lax
from jax.experimental import pallas as pl
from jax.experimental.pallas import tpu as pltpu
from jax.sharding import PartitionSpec as P

HEAD_DIM = 64
ITERS = 2
GROUPS = 2
X_TYPE = jnp.bfloat16
Z_TYPES = (jnp.bfloat16, jnp.float32)
EPS = 1e-06


def modulation(step_value, time_weight):
    channels = time_weight.shape[0]
    half_width = channels // 2
    frequency = jnp.exp(-math.log(10000.0) * jnp.arange(half_width, dtype=jnp.float32) / half_width)
    angles = step_value.astype(jnp.float32) * frequency
    encoded = jnp.concatenate([jnp.cos(angles), jnp.sin(angles)])[None, :]
    shifted = jnp.dot(
        encoded, time_weight, precision=lax.Precision.HIGHEST, preferred_element_type=jnp.float32
    )[0]
    return (1.0 + shifted[:channels], shifted[channels:])


def kernel(
    n_tm,
    n_frame,
    width,
    groups,
    start_ref,
    guess_ref,
    noise_ref,
    rows_ref,
    wconv_ref,
    wattn_ref,
    wout_ref,
    out_ref,
    state,
    taps,
    mixed,
    term,
    proj,
    ain,
    rin,
    aout,
    rout,
    pair_out,
    pair_in,
    zout_first,
    zout_last,
    zin_first,
    zin_last,
    back_out,
    back_in,
    in_send,
    in_recv,
    out_send,
    out_recv,
    pair_send,
    pair_recv,
    z_send,
    z_recv,
    back_send,
    back_recv,
):
    cells, channels = start_ref.shape
    share = cells // n_frame
    piece = share // groups
    half = piece // 2
    pieces = n_frame * groups
    me_tm = lax.axis_index("tm")
    me = lax.axis_index("frame")
    link = me_tm // 2
    side = lax.rem(me_tm, 2)
    links = n_tm // 2
    has_prev = link > 0
    has_next = link < links - 1

    def at_frame(f):
        return {"tm": me_tm, "frame": f}

    def at_tm(t):
        return {"tm": t, "frame": me}

    def peer(s):
        return lax.rem(me + s, n_frame)

    def sender(s):
        return lax.rem(me + n_frame - s, n_frame)

    barrier = pltpu.get_barrier_semaphore()

    def greet(device):
        pl.semaphore_signal(barrier, inc=1, device_id=device, device_id_type=pl.DeviceIdType.MESH)

    for s in range(1, n_frame):
        greet(at_frame(peer(s)))
    greet(at_tm(me_tm + 1 - 2 * side))

    @pl.when(has_prev)
    def _():
        greet(at_tm(me_tm - 2))

    @pl.when(has_next)
    def _():
        greet(at_tm(me_tm + 2))

    def meet():
        pl.semaphore_wait(barrier, n_frame + has_prev.astype(jnp.int32) + has_next.astype(jnp.int32))

    edge = jnp.zeros((width, 3 * channels), jnp.bfloat16)
    taps[0:width, :] = edge
    taps[cells + width : cells + 2 * width, :] = edge

    @pl.when(link == 0)
    def _():
        zin_first[...] = jnp.zeros_like(zin_first)
        zin_last[...] = jnp.zeros_like(zin_last)

    gain_space = rows_ref[0:1, :]
    offset = rows_ref[1:2, :]
    coefficient = rows_ref[2:3, :]
    time_value = rows_ref[3:4, :]
    gain_attention = rows_ref[4:5, :]

    def inverse_rms(v):
        return lax.rsqrt(jnp.mean(v * v, axis=-1, keepdims=True) + EPS)

    column = lax.broadcasted_iota(jnp.int32, (piece, channels), 0) % width
    head_in = lax.broadcasted_iota(jnp.int32, (2 * channels, channels), 0) % channels // HEAD_DIM
    head_to = lax.broadcasted_iota(jnp.int32, (2 * channels, channels), 1) // HEAD_DIM
    gather_heads = jnp.where(head_in == head_to, 1.0, 0.0).astype(jnp.bfloat16)

    def make_taps(at, x):
        normed = x * inverse_rms(x) * gain_space + offset
        left = jnp.where(column == 0, 0.0, pltpu.roll(normed, 1, 0))
        right = jnp.where(column == width - 1, 0.0, pltpu.roll(normed, piece - 1, 0))
        to = pl.multiple_of(at + width, width)
        taps[pl.ds(to, piece), 0:channels] = left.astype(jnp.bfloat16)
        taps[pl.ds(to, piece), channels : 2 * channels] = normed.astype(jnp.bfloat16)
        taps[pl.ds(to, piece), 2 * channels : 3 * channels] = right.astype(jnp.bfloat16)

    def first_taps(i, _):
        at = pl.multiple_of(i * piece, piece)
        make_taps(at, guess_ref[pl.ds(at, piece), :])
        return 0

    def remote(src, dst, send, recv, device):
        return pltpu.make_async_remote_copy(
            src_ref=src,
            dst_ref=dst,
            send_sem=send,
            recv_sem=recv,
            device_id=device,
            device_id_type=pl.DeviceIdType.MESH,
        )

    for turn in range(ITERS):
        source = guess_ref if turn == 0 else state
        zout, zin = (zout_last, zin_last) if turn == ITERS - 1 else (zout_first, zin_first)
        if turn == 0:
            lax.fori_loop(0, pieces, first_taps, 0)
            meet()

        def in_copy(s, g):
            return remote(
                ain.at[turn, g, peer(s)],
                rin.at[turn, g, me],
                in_send.at[turn, g, s],
                in_recv.at[turn, g, s],
                at_frame(peer(s)),
            )

        def out_copy(s, g):
            return remote(
                aout.at[turn, g, peer(s)],
                rout.at[turn, g, me],
                out_send.at[turn, g, s],
                out_recv.at[turn, g, s],
                at_frame(peer(s)),
            )

        def pair_copy(i):
            return remote(
                pair_out.at[turn, i],
                pair_in.at[turn, i],
                pair_send.at[turn, i],
                pair_recv.at[turn, i],
                at_tm(me_tm + 1 - 2 * side),
            )

        def z_copy(i):
            return remote(
                zout.at[turn, i], zin.at[turn, i], z_send.at[turn, i], z_recv.at[turn, i], at_tm(me_tm + 2)
            )

        def back_copy(i):
            return remote(
                back_out.at[turn, i],
                back_in.at[turn, i],
                back_send.at[turn, i],
                back_recv.at[turn, i],
                at_tm(me_tm + 1 - 2 * side),
            )

        def rows_of(q, g):
            return pl.multiple_of(q * share + g * piece, piece)

        def mix(g):
            everyone = range(n_frame)
            total = jnp.zeros((n_frame * piece, channels), jnp.float32)
            for row in range(3):
                near = [taps[pl.ds(rows_of(q, g) + row * width, piece), :] for q in everyone]
                total += jnp.dot(
                    jnp.concatenate(near, axis=0),
                    wconv_ref[row * 3 * channels : (row + 1) * 3 * channels, :],
                    preferred_element_type=jnp.float32,
                )
            here = jnp.concatenate([source[pl.ds(rows_of(q, g), piece), :] for q in everyone], axis=0)
            value = here + total / (1.0 + jnp.exp(-total))
            normed = (value * inverse_rms(value) * gain_attention).astype(jnp.bfloat16)
            for q in everyone:
                mixed[pl.ds(rows_of(q, g), piece), :] = value[q * piece : (q + 1) * piece]
                ain[turn, g, q] = normed[q * piece : (q + 1) * piece]

        def project(g, blocks, owners):
            result = (
                jnp.dot(jnp.concatenate(blocks, axis=0), wattn_ref[...], preferred_element_type=jnp.float32)
                .astype(jnp.bfloat16)
                .astype(jnp.float32)
            )
            for at, f in enumerate(owners):
                proj[g, f] = result[at * piece : (at + 1) * piece]

        def attend(f, g):
            query = proj[g, f, :, 0:channels]
            products = (query[None] * proj[g, :, :, channels : 2 * channels]).reshape(-1, channels)
            high = products.astype(jnp.bfloat16)
            low = (products - high.astype(jnp.float32)).astype(jnp.bfloat16)
            scores = jnp.dot(
                jnp.concatenate([high, low], axis=-1), gather_heads, preferred_element_type=jnp.float32
            ).reshape(n_frame, piece, channels) * (1.0 / math.sqrt(HEAD_DIM))
            raised = jnp.exp(scores - jnp.max(scores, axis=0, keepdims=True))
            weights = raised * (1.0 / jnp.sum(raised, axis=0, keepdims=True))
            weights = weights.astype(jnp.bfloat16).astype(jnp.float32)
            aout[turn, g, f] = jnp.sum(weights * proj[g, :, :, 2 * channels : 3 * channels], axis=0).astype(
                jnp.bfloat16
            )

        def close(g, blocks, owners):
            result = jnp.dot(
                jnp.concatenate(blocks, axis=0), wout_ref[...], preferred_element_type=jnp.float32
            )
            for at, q in enumerate(owners):
                rows = pl.ds(rows_of(q, g), piece)
                drift = mixed[rows, :] + result[at * piece : (at + 1) * piece]
                term[rows, :] = coefficient * (drift + time_value * noise_ref[rows, :])

        def share_pairs(g, steps):
            for s in steps:
                other = pl.multiple_of(rows_of(sender(s), g) + (1 - side) * half, half)
                pair_out[turn, g * n_frame + s] = term[pl.ds(other, half), :].astype(pair_out.dtype)
            for s in steps:
                pair_copy(g * n_frame + s).start()

        def place(i):
            return pl.multiple_of(sender(i % n_frame) * share + i // n_frame * piece, piece)

        others = range(1, n_frame)
        for g in range(groups):
            mix(g)
            for s in others:
                in_copy(s, g).start()
        for g in range(groups):
            project(g, [ain[turn, g, me]], [me])

        for g in range(groups):
            for s in others:
                in_copy(s, g).wait_recv()
            project(g, [rin[turn, g, sender(s)] for s in others], [sender(s) for s in others])

            def attend_and_send(s, _):
                attend(peer(s), g)
                out_copy(s, g).start()
                return 0

            lax.fori_loop(1, n_frame, attend_and_send, 0)
            attend(me, g)

        for g in range(groups):
            close(g, [aout[turn, g, me]], [me])
            share_pairs(g, [0])
            for s in others:
                out_copy(s, g).wait_recv()
            close(g, [rout[turn, g, sender(s)] for s in others], [sender(s) for s in others])
            share_pairs(g, others)

        def chain(i, _):
            own = pl.multiple_of(place(i) + side * half, half)
            mine = term[pl.ds(own, half), :]
            pair_copy(i).wait_recv()
            both = mine + pair_in[turn, i].astype(jnp.float32)

            @pl.when(has_prev)
            def _():
                z_copy(i).wait_recv()

            earlier = zin[turn, i].astype(jnp.float32)

            @pl.when(has_next)
            def _():
                zout[turn, i] = (earlier + both).astype(zout.dtype)
                z_copy(i).start()

            back_out[turn, i] = jnp.where(side == 0, earlier + mine, earlier).astype(back_out.dtype)
            back_copy(i).start()
            return 0

        def finish(i, _):
            at = place(i)
            own = pl.multiple_of(at + side * half, half)
            other = pl.multiple_of(at + (1 - side) * half, half)
            last = turn == ITERS - 1
            base, target = (term, out_ref) if last else (start_ref, state)
            earlier = zin[turn, i].astype(jnp.float32)
            first = jnp.where(side == 0, earlier, earlier + pair_in[turn, i].astype(jnp.float32))
            target[pl.ds(own, half), :] = base[pl.ds(own, half), :] + first
            back_copy(i).wait_recv()
            target[pl.ds(other, half), :] = base[pl.ds(other, half), :] + back_in[turn, i].astype(jnp.float32)
            if not last:
                make_taps(at, state[pl.ds(at, piece), :])
            return 0

        def chain_and_finish(i, _):
            chain(i, 0)
            finish(i - LAG, 0)
            return 0

        lax.fori_loop(0, pieces, chain, 0)
        lax.fori_loop(0, pieces, finish, 0)

        def sent(i, _):
            pair_copy(i).wait_send()
            back_copy(i).wait_send()

            @pl.when(has_next)
            def _():
                z_copy(i).wait_send()

            return 0

        lax.fori_loop(0, pieces, sent, 0)

        for g in range(groups):

            def left(s, _):
                in_copy(s, g).wait_send()
                out_copy(s, g).wait_send()
                return 0

            lax.fori_loop(1, n_frame, left, 0)


def shards(
    n_tm,
    n_frame,
    start_state,
    initial_guess,
    noise_draws,
    timesteps,
    gain_space,
    gain_attention,
    time_weight,
    space_weight,
    attention_weight,
    output_weight,
):
    _, height, width, channels = start_state.shape
    cells = height * width
    share = cells // n_frame
    groups = GROUPS if share // width % GROUPS == 0 else 1
    piece = share // groups
    pieces = n_frame * groups
    step_value = timesteps[0]
    time_value = step_value.astype(jnp.float32) / 1000.0
    coefficient = (0.5 + time_value) / math.sqrt(n_tm)
    scaling, offset = modulation(step_value, time_weight)
    rows = jnp.stack(
        [
            gain_space * scaling,
            offset,
            jnp.full((channels,), coefficient),
            jnp.full((channels,), time_value),
            gain_attention,
        ]
    )
    vmem = pl.BlockSpec(memory_space=pltpu.VMEM)
    f32, bf16 = jnp.float32, jnp.bfloat16
    dma = pltpu.SemaphoreType.DMA
    exchange = pltpu.VMEM((ITERS, groups, n_frame, piece, channels), bf16)
    cross = pltpu.VMEM((ITERS, pieces, piece // 2, channels), X_TYPE)
    along = [pltpu.VMEM((ITERS, pieces, piece // 2, channels), kind) for kind in Z_TYPES]
    total = pl.pallas_call(
        functools.partial(kernel, n_tm, n_frame, width, groups),
        out_shape=jax.ShapeDtypeStruct((cells, channels), f32),
        in_specs=[vmem] * 7,
        out_specs=vmem,
        scratch_shapes=[
            pltpu.VMEM((cells, channels), f32),
            pltpu.VMEM((cells + 2 * width, 3 * channels), bf16),
            pltpu.VMEM((cells, channels), f32),
            pltpu.VMEM((cells, channels), f32),
            pltpu.VMEM((groups, n_frame, piece, 3 * channels), f32),
            exchange,
            exchange,
            exchange,
            exchange,
            cross,
            cross,
            *along,
            *along,
            cross,
            cross,
            *([dma((ITERS, groups, n_frame))] * 4),
            *([dma((ITERS, pieces))] * 6),
        ],
        compiler_params=pltpu.CompilerParams(collective_id=0, has_side_effects=True),
    )(
        start_state.reshape(cells, channels),
        initial_guess.reshape(cells, channels),
        noise_draws.reshape(cells, channels),
        rows,
        space_weight,
        attention_weight,
        output_weight,
    )
    return start_state[None] + total.reshape(1, 1, height, width, channels)


def solution(mesh):
    return jax.shard_map(
        functools.partial(shards, mesh.shape["tm"], mesh.shape["frame"]),
        mesh=mesh,
        in_specs=(
            P("frame", None, None, None),
            P("tm", "frame", None, None, None),
            P("tm", "frame", None, None, None),
            P("tm"),
            P(),
            P(),
            P(),
            P(),
            P(),
            P(),
        ),
        out_specs=P("tm", "frame", None, None, None),
        check_vma=False,
    )
```
